32 devices in a mesh: row: 4 (over y, x), col: 8 (over z, core).
Axes of the slice: x: 2, y: 2, z: 4, core: 2. Of those that a mesh axis runs over, the one named last changes fastest.
Arguments:
- trailing_grad: bfloat16 [4, 8, 768, 24576], P(None, 'col', None, 'row'), may hold values from -6 to 6
- panel: bfloat16 [24576, 512], P(('row', 'col')), may hold values from -0.0390625 to 0.0390625
- panel_grad: float32 [24576, 512], P(('row', 'col')), may hold values from -6 to 6
- diag_factor: float32 [512, 512], replicated, may hold values from -2 to 2, as said below
- diag_grad: float32 [512, 512], replicated, may hold values from -6 to 6
Outputs:
- panel_adj: float32 [24576, 512], P(('row', 'col'))
- diag_adj: float32 [512, 512], replicated
The draws below stay inside these ranges and needn't reach their ends.
Inputs may be any that keep to these rules, and one draw needn't show every extreme that they name: `diag_factor`: lower triangular with zeros above the diagonal; diagonal entries between 1 and 2.
All inputs are finite; a program needn't handle non-finite values.
Results may differ from the reference program's by a relative error of at most 0.0003.
Values may be sent and summed in bfloat16 or wider, within the bound.
A program may use at most 128 MiB of HBM per device.

```python
import jax
import jax.numpy as jnp
from jax import lax

M = 24576
B = 512
GROUP = 768
N_ROW = 4
N_COL = 8


def draw_diag_factor(key, part):
    base = jax.random.fold_in(key, 7)
    key_diag, key_off = jax.random.split(base)
    diagonal = jax.random.uniform(key_diag, (B,), jnp.float32, 1.0, 2.0)
    off = jax.random.normal(key_off, (B, B), jnp.float32)
    off = jnp.clip(off * (0.6 / jnp.sqrt(B * 1.0)), -1.0, 1.0)
    rows = lax.broadcasted_iota(jnp.int32, (B, B), 0)
    cols = lax.broadcasted_iota(jnp.int32, (B, B), 1)
    strict = jnp.where(rows > cols, off, 0.0)
    return strict + jnp.diag(diagonal)


def strengthened(values, key, source, target, parts, factor):
    def block_of(dim):
        return (jnp.arange(values.shape[dim]) // (values.shape[dim] // parts)).reshape((-1,) + (1,) * (values.ndim - 1 - dim))

    one_side = jax.random.permutation(key, parts)[block_of(target)]
    second = (block_of(target) + parts // 2) % parts
    return jnp.where((block_of(source) == one_side) | (block_of(source) == second), factor * values, values)


def steps_of(rng, shape, shards, low, top_value):
    loudness, own = 1.0, jax.random.fold_in(rng, 6)
    for axis_at, parts in shards:
        steps = jnp.exp(jax.random.uniform(jax.random.fold_in(own, axis_at), (parts,), jnp.float32, low / len(shards), top_value / len(shards)))
        loudness = loudness * jnp.repeat(steps, shape[axis_at] // parts).reshape([-1 if axis == axis_at else 1 for axis in range(len(shape))])
    return loudness


def centred(stream_key, extent, deviation, most, pieces=(), held_as=jnp.bfloat16):
    array = jax.random.normal(stream_key, extent, jnp.float32) * deviation
    if len(pieces) > 0:
        array = steps_of(stream_key, extent, pieces, -0.22, 0.18) * array
    return jnp.clip(array, min=-most, max=most).astype(held_as)


def noise_with(rng, shape, spread, most, cuts, heavy, kind=jnp.bfloat16):
    entries = spread * jax.random.normal(rng, shape, jnp.float32)
    if cuts:
        entries = entries * steps_of(rng, shape, cuts, -0.22, 0.18)
    return jnp.clip(strengthened(entries, jax.random.fold_in(rng, 3), *heavy), -most, most).astype(kind)


def setup_inputs(seed: int = 0) -> dict:
    key_of = jax.random.split(jax.random.key(seed), 6)
    return {
        "trailing_grad": noise_with(key_of[0], (N_ROW, N_COL, GROUP, M), 1.0, 6.0, ((1, 8), (3, 4)), (1, 3, 8, 2.0)),
        "panel": centred(key_of[1], (M, B), M ** -0.5, 0.0390625, ((0, 32),)),
        "panel_grad": centred(key_of[2], (M, B), 1.0, 6.0, ((0, 32),), jnp.float32),
        "diag_factor": draw_diag_factor(jax.random.fold_in(key_of[5], 71), 0),
        "diag_grad": centred(key_of[4], (B, B), 1.0, 6.0, (), jnp.float32),
    }


def halve_lower(matrix):
    rows = lax.broadcasted_iota(jnp.int32, matrix.shape, 0)
    cols = lax.broadcasted_iota(jnp.int32, matrix.shape, 1)
    keep = jnp.where(rows > cols, 1.0, jnp.where(rows == cols, 0.5, 0.0)).astype(matrix.dtype)
    return matrix * keep

def adjoint_block(diag_new, lower):
    inner = halve_lower(jnp.dot(lower.T, jnp.tril(diag_new), precision=lax.Precision.HIGHEST))
    left = jax.scipy.linalg.solve_triangular(lower, inner, lower=True, trans=1)
    right = jax.scipy.linalg.solve_triangular(lower, left.T, lower=True, trans=1).T
    return 0.5 * (right + right.T)

def reference(trailing_grad, panel, panel_grad, diag_factor, diag_grad):
    flipped = trailing_grad.reshape(M, M)
    direct = lax.dot_general(flipped.astype(jnp.float32), panel.astype(jnp.float32), (((0,), (0,)), ((), ())), preferred_element_type=jnp.float32)
    transposed = jnp.dot(flipped.astype(jnp.float32), panel.astype(jnp.float32), preferred_element_type=jnp.float32)
    reduced = panel_grad - direct - transposed
    lower = jnp.tril(diag_factor)
    panel_adj = jax.scipy.linalg.solve_triangular(lower, reduced.T, lower=True, trans=1).T
    contrib = lax.dot_general(panel_adj, panel.astype(jnp.float32), (((0,), (0,)), ((), ())), precision=lax.Precision.HIGHEST)
    diag_new = diag_grad - contrib
    return (panel_adj, adjoint_block(diag_new, lower))
```

```python
import functools

import jax
import jax.numpy as jnp
from jax import lax
from jax.experimental import pallas as pl
from jax.experimental.pallas import tpu as pltpu
from jax.sharding import PartitionSpec as P

F32, BF16 = jnp.float32, jnp.bfloat16
VMEM_LIMIT = 66_000_000
NB = 4
BLK = 128
HI = lax.Precision.HIGHEST


def dot(a, b, ca=1, cb=0, precision=None):
    return lax.dot_general(
        a, b, (((ca,), (cb,)), ((), ())), precision=precision, preferred_element_type=F32
    )


def invert_blocks(l_ref, inv_ref):
    rows = lax.broadcasted_iota(jnp.int32, (BLK, BLK), 0)
    cols = lax.broadcasted_iota(jnp.int32, (BLK, BLK), 1)
    count = l_ref.shape[0] // BLK
    for j in range(count):
        block = l_ref[j * BLK : (j + 1) * BLK, j * BLK : (j + 1) * BLK]
        inv_ref[j] = jnp.where(rows == cols, 1.0 / jnp.where(rows == cols, block, 1.0), 0.0)

    def level(k, carry):
        same = (rows >> (k + 1)) == (cols >> (k + 1))
        mask = same & (((rows >> k) & 1) == 1) & (((cols >> k) & 1) == 0)
        for j in range(count):
            block = l_ref[j * BLK : (j + 1) * BLK, j * BLK : (j + 1) * BLK]
            x = inv_ref[j]
            y = dot(jnp.where(mask, block, 0.0), x, precision=HI)
            inv_ref[j] = x - dot(x, y, precision=HI)
        return carry

    lax.fori_loop(0, BLK.bit_length() - 1, level, 0)


def main_kernel(
    n_row, n_col, G, panel, panel_t, pg, low,
    dt_out, t_out, q_out, inv_out, pr, rl, tr,
    colp, rowp, gbuf, tacc, dsum, dpart, stage,
    gsem, cs, cr, zs, zr, ps, prr, ds, dr, rs, rr, ts, trs, lsem,
):
    nz = n_col // 2
    r, c = lax.axis_index("row"), lax.axis_index("col")
    z, k = c // 2, c % 2
    other = 2 * z + 1 - k
    g = panel.shape[0]
    last = nz - 1

    def dev(row, col):
        return dict(device_id=(row, col), device_id_type=pl.DeviceIdType.MESH)

    def tile_of(s):
        t = s - 2 * n_row
        i = t // n_row
        z_d = z_order(i // 2)
        c_d = 2 * z_d + jnp.where(i % 2 == 0, 1 - k, k)
        u = t - n_row * n_col
        rest = n_col - 2
        v = jnp.maximum(u, 0)
        a_b = (r + 1 + v // rest) % n_row
        jj = v % rest
        c_b = 2 * ((z + 1 + jj // 2) % nz) + jj % 2
        a = jnp.where(u >= 0, a_b, jnp.where(t >= 0, jnp.maximum(t, 0) % n_row, s % n_row))
        col = jnp.where(u >= 0, c_b, jnp.where(t >= 0, c_d, jnp.where(s < n_row, c, other)))
        return a, col

    def z_order(i):
        i = jnp.clip(i, 0, last)
        return jnp.where(z < nz // 2, last - i, i)

    total = 2 * n_row * n_col

    def tile_copy(s):
        a, col = tile_of(s)
        return pltpu.make_async_copy(
            G.at[pl.ds(pl.multiple_of(a * g, g), g), pl.ds(pl.multiple_of(col * g, g), g)],
            gbuf.at[s % NB],
            gsem.at[s % NB],
        )

    def next_tile(s):
        tile_copy(s).wait()

        @pl.when(s + NB - 1 < total)
        def _():
            tile_copy(s + NB - 1).start()

        a, col = tile_of(s)
        return a, col, gbuf[s % NB]

    for s in range(NB - 1):
        tile_copy(s).start()

    barrier = pltpu.get_barrier_semaphore()
    for d in range(1, n_row):
        pl.semaphore_signal(barrier, inc=1, **dev((r + d) % n_row, c))
    pl.semaphore_signal(barrier, inc=1, **dev(r, other))

    @pl.when(z > 0)
    def _():
        pl.semaphore_signal(barrier, inc=1, **dev(r, c - 2))

    @pl.when(z < last)
    def _():
        pl.semaphore_signal(barrier, inc=1, **dev(r, c + 2))

    near = jnp.where(z > 0, 1, 0) + jnp.where(z < last, 1, 0)
    pl.semaphore_wait(barrier, n_row + near)

    def col_send(d):
        return pltpu.make_async_remote_copy(
            panel_t, colp.at[r], cs.at[d], cr.at[d], **dev((r + d) % n_row, c)
        )

    def block_send(h, way, src):
        zb = z - (h - 1) if way == 0 else z + (h - 1)
        slot = 2 * zb + k
        return pltpu.make_async_remote_copy(
            rowp.at[slot] if src is None else src,
            rowp.at[slot],
            zs.at[way, h],
            zr.at[way, h],
            **dev(r, c + 2 if way == 0 else c - 2),
        )

    def pair_send(zb, src):
        slot = 2 * zb + k
        return pltpu.make_async_remote_copy(
            rowp.at[slot] if src is None else src, rowp.at[slot], ps.at[zb], prr.at[zb], **dev(r, other)
        )

    pair_send(z, panel).start()

    @pl.when(z < last)
    def _():
        block_send(1, 0, panel).start()

    @pl.when(z > 0)
    def _():
        block_send(1, 1, panel).start()

    for d in range(1, n_row):
        col_send(d).start()

    def relay(h):
        for way in range(2):
            zb = z - h if way == 0 else z + h
            have = (zb >= 0) if way == 0 else (zb <= last)
            onward = (z < last) if way == 0 else (z > 0)

            @pl.when(have)
            def _():
                pltpu.make_async_remote_copy(
                    panel, rowp.at[2 * zb + k], zs.at[way, h], zr.at[way, h], **dev(r, other)
                ).wait_recv()
                pair_send(zb, None).start()

                @pl.when(onward)
                def _():
                    block_send(h + 1, way, None).start()

    rowp[c] = panel[...]
    colp[r] = panel_t[...]

    def zero(a, carry):
        tacc[a] = jnp.zeros((g, panel.shape[1]), F32)
        return carry

    lax.fori_loop(0, n_row, zero, 0)

    def t_step(s, carry):
        a, col, tile = next_tile(s)
        tacc[a] += dot(tile, rowp[col])
        return carry

    lax.fori_loop(0, n_row, t_step, 0)

    def pair_wait(zb):
        pltpu.make_async_remote_copy(
            panel, rowp.at[2 * zb + 1 - k], ps.at[zb], prr.at[zb], **dev(r, other)
        ).wait_recv()

    pair_wait(z)
    lax.fori_loop(n_row, 2 * n_row, t_step, 0)
    invert_blocks(low, inv_out)
    relay(1)
    for d in range(1, n_row):
        pltpu.make_async_remote_copy(
            panel_t, colp.at[(r + n_row - d) % n_row], cs.at[d], cr.at[d], **dev((r + d) % n_row, c)
        ).wait_recv()

    def part_send(zb, slot):
        return pltpu.make_async_remote_copy(
            dpart.at[slot], pr.at[zb], ds.at[slot], dr.at[zb], **dev(r, other)
        )

    def sum_send(way, zb):
        return pltpu.make_async_remote_copy(
            dsum.at[zb], rl.at[way, zb], rs.at[way, zb], rr.at[way, zb],
            **dev(r, c + 2 if way == 0 else c - 2),
        )

    def add_in(dst, src):
        cp = pltpu.make_async_copy(src, stage, lsem)
        cp.start()
        cp.wait()
        dst[...] += stage[...]

    def presum(i):
        zb = z_order(i)
        part_send(zb, i % 2).wait_recv()
        add_in(dsum.at[zb], pr.at[zb])

        @pl.when((z == 0) & (zb > 0))
        def _():
            sum_send(0, zb).start()

        @pl.when((z == last) & (zb < last))
        def _():
            sum_send(1, zb).start()

    def d_into(base, ref):
        def step(j, carry):
            a, col, tile = next_tile(base + j)
            part = dot(colp[a], tile)

            @pl.when(j == 0)
            def _():
                ref[...] = part

            @pl.when(j > 0)
            def _():
                ref[...] += part

            return carry

        lax.fori_loop(0, n_row, step, 0)

    base = 2 * n_row
    for i in range(nz):
        zb = z_order(i)
        slot = i % 2
        if i >= 2:
            part_send(z_order(i - 2), slot).wait_send()
        d_into(base + 2 * i * n_row, dpart.at[slot])
        part_send(zb, slot).start()
        d_into(base + (2 * i + 1) * n_row, dsum.at[zb])
        presum(i)
        if i + 2 < nz:
            relay(i + 2)
    for h in range(nz + 1, nz):
        relay(h)

    def wait_others(d, carry):
        pair_wait((z + d) % nz)
        return carry

    lax.fori_loop(1, nz, wait_others, 0)

    def t_send(d):
        a = (r + d) % n_row
        return pltpu.make_async_remote_copy(
            tacc.at[a], tr.at[r], ts.at[d], trs.at[d], **dev(a, c)
        )

    base = 2 * n_row + n_row * n_col
    rest = n_col - 2
    for i in range(n_row):
        lax.fori_loop(base + i * rest, base + (i + 1) * rest, t_step, 0)
        if i < n_row - 1:
            t_send(i + 1).start()

    q_out[...] = jnp.zeros(q_out.shape, F32)

    def q_step(a, carry):
        t = tacc[a]
        hi = t.astype(BF16)
        lo = (t - hi.astype(F32)).astype(BF16)
        q_out[...] += dot(colp[a], hi) + dot(colp[a], lo)
        return carry

    lax.fori_loop(0, n_row, q_step, 0)

    def hop(way, zb):
        sum_wait = pltpu.make_async_remote_copy(
            stage, rl.at[way, zb], rs.at[way, zb], rr.at[way, zb], **dev(r, other)
        )
        sum_wait.wait_recv()
        add_in(dsum.at[zb], rl.at[way, zb])

    for q in range(nz):
        up = last - q

        @pl.when((z > 0) & (up > z))
        def _():
            hop(0, up)
            sum_send(0, up).start()

        @pl.when((z < last) & (q < z))
        def _():
            hop(1, q)
            sum_send(1, q).start()

    def fetch(src, dst):
        cp = pltpu.make_async_copy(src, dst, lsem)
        cp.start()
        cp.wait()

    t_out[...] = pg[...] - tacc[r]
    tbuf = tacc.at[(r + 1) % n_row]
    for d in range(1, n_row):
        t_send(d).wait_send()
    for d in range(1, n_row):
        src = (r + n_row - d) % n_row
        pltpu.make_async_remote_copy(
            tacc.at[src], tr.at[src], ts.at[d], trs.at[d], **dev((r + d) % n_row, c)
        ).wait_recv()
        fetch(tr.at[src], tbuf)
        t_out[...] -= tbuf[...]

    @pl.when(z > 0)
    def _():
        hop(0, z)

    @pl.when(z < last)
    def _():
        hop(1, z)

    dt_out[...] = dsum[z]

    for d in range(1, n_row):
        col_send(d).wait_send()
    for way in range(2):
        for h in range(1, nz):
            zb = z - (h - 1) if way == 0 else z + (h - 1)
            sent = ((zb >= 0) & (z < last)) if way == 0 else ((zb <= last) & (z > 0))

            @pl.when(sent)
            def _():
                block_send(h, way, panel).wait_send()

    for zb in range(nz):
        pair_send(zb, panel).wait_send()
        sent_up = z < zb
        sent_down = z > zb

        @pl.when(sent_up)
        def _():
            sum_send(0, zb).wait_send()

        @pl.when(sent_down)
        def _():
            sum_send(1, zb).wait_send()

    for i in range(max(nz - 2, 0), nz):
        part_send(z_order(i), i % 2).wait_send()


def main_call(G, panel, pg, low, n_row, n_col):
    g, b = panel.shape
    nz = n_col // 2
    vm = pl.BlockSpec(memory_space=pltpu.VMEM)
    hbm = pl.BlockSpec(memory_space=pl.ANY)
    dma = pltpu.SemaphoreType.DMA
    sds = jax.ShapeDtypeStruct
    sizes = [(NB,), (n_row,), (n_row,), (2, nz + 1), (2, nz + 1), (nz,), (nz,), (2,), (nz,),
             (2, nz), (2, nz), (n_row,), (n_row,)]
    flops = 4 * G.shape[0] * G.shape[1] * b
    outs = pl.pallas_call(
        functools.partial(main_kernel, n_row, n_col),
        out_shape=[
            sds((b, g), F32), sds((g, b), F32), sds((b, b), F32), sds((b // BLK, BLK, BLK), F32),
            sds((nz, b, g), F32), sds((2, nz, b, g), F32), sds((n_row, g, b), F32),
        ],
        in_specs=[hbm, vm, vm, vm, vm],
        out_specs=[vm, vm, vm, vm, hbm, hbm, hbm],
        scratch_shapes=[
            pltpu.VMEM((n_row, b, g), BF16),
            pltpu.VMEM((n_col, g, b), BF16),
            pltpu.VMEM((NB, g, g), BF16),
            pltpu.VMEM((n_row, g, b), F32),
            pltpu.VMEM((nz, b, g), F32),
            pltpu.VMEM((2, b, g), F32),
            pltpu.VMEM((b, g), F32),
        ]
        + [dma(s) for s in sizes]
        + [dma],
        compiler_params=pltpu.CompilerParams(
            collective_id=0, has_side_effects=True, vmem_limit_bytes=VMEM_LIMIT
        ),
        cost_estimate=pl.CostEstimate(flops=flops, bytes_accessed=4 * G.size, transcendentals=0),
    )(G, panel, panel.T, pg, low)
    return outs[:4]


def sum_kernel(n_row, n_col, x, out, a_in, a_sum, b_in, s1, r1, s2, r2, s3, r3, s4, r4):
    r, c = lax.axis_index("row"), lax.axis_index("col")

    def dev(row, col):
        return dict(device_id=(row, col), device_id_type=pl.DeviceIdType.MESH)

    def row_at(d):
        return lax.rem(r + d, n_row)

    def col_at(d):
        return lax.rem(c + d, n_col)

    barrier = pltpu.get_barrier_semaphore()
    for d in range(1, n_row):
        pl.semaphore_signal(barrier, inc=1, **dev(row_at(d), c))
    for d in range(1, n_col):
        pl.semaphore_signal(barrier, inc=1, **dev(r, col_at(d)))
    pl.semaphore_wait(barrier, n_row + n_col - 2)

    remote = pltpu.make_async_remote_copy
    one = [
        remote(x.at[row_at(d)], a_in.at[d], s1.at[d], r1.at[d], **dev(row_at(d), c))
        for d in range(1, n_row)
    ]
    for cp in one:
        cp.start()
    a_sum[...] = x[r]
    for cp, d in zip(one, range(1, n_row)):
        cp.wait_recv()
        a_sum[...] += a_in[d]
    two = [
        remote(a_sum.at[col_at(d)], b_in.at[d], s2.at[d], r2.at[d], **dev(r, col_at(d)))
        for d in range(1, n_col)
    ]
    for cp in two:
        cp.start()
    acc = a_sum[c]
    for cp, d in zip(two, range(1, n_col)):
        cp.wait_recv()
        acc += b_in[d]
    out[r, c] = acc
    three = [
        remote(out.at[r, c], out.at[r, c], s3.at[d], r3.at[d], **dev(r, col_at(d)))
        for d in range(1, n_col)
    ]
    for cp in three:
        cp.start()
    for d in range(1, n_col):
        remote(
            out.at[r, c], out.at[r, col_at(n_col - d)], s3.at[d], r3.at[d], **dev(r, col_at(d))
        ).wait_recv()
    four = [
        remote(out.at[r], out.at[r], s4.at[d], r4.at[d], **dev(row_at(d), c))
        for d in range(1, n_row)
    ]
    for cp in four:
        cp.start()
    for d in range(1, n_row):
        remote(
            out.at[r], out.at[row_at(n_row - d)], s4.at[d], r4.at[d], **dev(row_at(d), c)
        ).wait_recv()
    for cp in one + two + three + four:
        cp.wait_send()


def sum_call(x, n_row, n_col):
    shape = x.shape
    w = x.size // (n_row * n_col * 8)
    x = x.reshape(n_row, n_col, 8, w)
    vm = pl.BlockSpec(memory_space=pltpu.VMEM)
    dma = pltpu.SemaphoreType.DMA
    row, col = dma((n_row,)), dma((n_col,))
    out = pl.pallas_call(
        functools.partial(sum_kernel, n_row, n_col),
        out_shape=jax.ShapeDtypeStruct(x.shape, F32),
        in_specs=[vm],
        out_specs=vm,
        scratch_shapes=[
            pltpu.VMEM((n_row, n_col, 8, w), F32),
            pltpu.VMEM((n_col, 8, w), F32),
            pltpu.VMEM((n_col, 8, w), F32),
            row, row, col, col, col, col, row, row,
        ],
        compiler_params=pltpu.CompilerParams(collective_id=1, has_side_effects=True),
    )(x)
    return out.reshape(shape)


def right_blocks(rhs, low, inv):
    n = low.shape[0] // BLK
    part = lambda j: slice(j * BLK, (j + 1) * BLK)
    xs = [None] * n
    for j in reversed(range(n)):
        acc = rhs[:, part(j)]
        if j < n - 1:
            done = jnp.concatenate(xs[j + 1 :], axis=1)
            acc = acc - dot(done, low[(j + 1) * BLK :, part(j)], precision=HI)
        xs[j] = dot(acc, inv[j], precision=HI)
    return jnp.concatenate(xs, axis=1)


def left_blocks(rhs, low, inv):
    n = low.shape[0] // BLK
    part = lambda j: slice(j * BLK, (j + 1) * BLK)
    xs = [None] * n
    for j in reversed(range(n)):
        acc = rhs[part(j), :]
        if j < n - 1:
            done = jnp.concatenate(xs[j + 1 :], axis=0)
            acc = acc - dot(low[(j + 1) * BLK :, part(j)], done, 0, 0, precision=HI)
        xs[j] = dot(inv[j], acc, 0, 0, precision=HI)
    return jnp.concatenate(xs, axis=0)


def panel_kernel(t_ref, dt_ref, low, inv, out):
    out[...] = right_blocks(t_ref[...] - dt_ref[...].T, low[...], inv[...])


def diag_kernel(s_ref, dg, low, inv, out):
    lower, inverse = low[...], inv[...]
    rows = lax.broadcasted_iota(jnp.int32, lower.shape, 0)
    cols = lax.broadcasted_iota(jnp.int32, lower.shape, 1)
    diag_new = dg[...] - left_blocks(s_ref[...], lower, inverse)
    inner = dot(lower, jnp.where(rows >= cols, diag_new, 0.0), 0, 0, precision=HI)
    inner = inner * jnp.where(rows > cols, 1.0, jnp.where(rows == cols, 0.5, 0.0))
    right = right_blocks(left_blocks(inner, lower, inverse), lower, inverse)
    out[...] = 0.5 * (right + right.T)


def local_call(body, shape, *args):
    vm = pl.BlockSpec(memory_space=pltpu.VMEM)
    return pl.pallas_call(
        body,
        out_shape=jax.ShapeDtypeStruct(shape, F32),
        in_specs=[vm] * len(args),
        out_specs=vm,
        compiler_params=pltpu.CompilerParams(vmem_limit_bytes=48_000_000),
    )(*args)


def plain_products(block, panel, panel_grad, lower):
    col_panel = lax.all_gather(panel, "row", axis=0, tiled=True)
    row_panel = lax.all_gather(panel, "col", axis=0, tiled=True)
    direct = lax.psum_scatter(dot(block, col_panel, 0, 0), "col", scatter_dimension=0, tiled=True)
    part = dot(block, row_panel)
    transposed = lax.psum_scatter(part, "row", scatter_dimension=0, tiled=True)
    high = part.astype(BF16)
    q = dot(col_panel, high, 0, 0) + dot(col_panel, (part - high.astype(F32)).astype(BF16), 0, 0)
    inv = local_call(invert_blocks, (lower.shape[0] // BLK, BLK, BLK), lower)
    return direct.T, panel_grad - transposed, q, inv


def on_device(n_row, n_col, trailing_grad, panel, panel_grad, diag_factor, diag_grad):
    local_flip = trailing_grad.reshape(-1, trailing_grad.shape[3])
    lower = jnp.tril(diag_factor)
    own = dot(panel_grad, panel.astype(F32), 0, 0, precision=HI)
    if panel.shape[0] % 128 == 0 and n_col % 2 == 0 and n_col > 2:
        dt, t, q, inv = main_call(local_flip, panel, panel_grad, lower, n_row, n_col)
    else:
        dt, t, q, inv = plain_products(local_flip, panel, panel_grad, lower)
    total = sum_call(own - q - q.T, n_row, n_col)
    panel_adj = local_call(panel_kernel, panel_grad.shape, t, dt, lower, inv)
    diag_adj = local_call(diag_kernel, lower.shape, total, diag_grad, lower, inv)
    return (panel_adj, diag_adj)


def solution(mesh):
    in_specs = (
        P(None, "col", None, "row"),
        P(("row", "col"), None),
        P(("row", "col"), None),
        P(),
        P(),
    )
    out_specs = (P(("row", "col"), None), P())
    body = functools.partial(on_device, mesh.shape["row"], mesh.shape["col"])
    return jax.shard_map(body, mesh=mesh, in_specs=in_specs, out_specs=out_specs, check_vma=False)
```

```python
import functools

import jax
import jax.numpy as jnp
from jax import lax
from jax.experimental import pallas as pl
from jax.experimental.pallas import tpu as pltpu
from jax.sharding import PartitionSpec as P

F32, BF16 = jnp.float32, jnp.bfloat16
VMEM_LIMIT = 66_000_000
NB = 4
EARLY = 2
BLK = 128
HI = lax.Precision.HIGHEST


def dot(a, b, ca=1, cb=0, precision=None):
    return lax.dot_general(
        a, b, (((ca,), (cb,)), ((), ())), precision=precision, preferred_element_type=F32
    )


def lower_blocks(count):
    return [(i, j) for i in range(count) for j in range(i + 1)]


def invert_blocks(l_ref, inv_ref):
    rows = lax.broadcasted_iota(jnp.int32, (BLK, BLK), 0)
    cols = lax.broadcasted_iota(jnp.int32, (BLK, BLK), 1)
    count = l_ref.shape[0] // BLK
    for j in range(count):
        block = l_ref[j * BLK : (j + 1) * BLK, j * BLK : (j + 1) * BLK]
        inv_ref[j] = jnp.where(rows == cols, 1.0 / jnp.where(rows == cols, block, 1.0), 0.0)

    def level(k, carry):
        same = (rows >> (k + 1)) == (cols >> (k + 1))
        mask = same & (((rows >> k) & 1) == 1) & (((cols >> k) & 1) == 0)
        for j in range(count):
            block = l_ref[j * BLK : (j + 1) * BLK, j * BLK : (j + 1) * BLK]
            x = inv_ref[j]
            y = dot(jnp.where(mask, block, 0.0), x, precision=HI)
            inv_ref[j] = x - dot(x, y, precision=HI)
        return carry

    lax.fori_loop(0, BLK.bit_length() - 1, level, 0)


def main_kernel(
    n_row, n_col, G, panel, panel_t, pg, low,
    dg, adj_out, diag_out, pr, rl, tr,
    colp, rowp, gbuf, tacc, dsum, dpart, stage, q_out, inv_out, own_t, sx, s_in, s_row, s_col, s_all,
    gsem, cs, cr, zs, zr, ps, prr, ds, dr, rs, rr, ts, trs, s1, r1, s2, r2, s3, r3, s4, r4, lsem,
):
    nz = n_col // 2
    r, c = lax.axis_index("row"), lax.axis_index("col")
    z, k = c // 2, c % 2
    other = 2 * z + 1 - k
    g = panel.shape[0]
    last = nz - 1

    def dev(row, col):
        return dict(device_id=(row, col), device_id_type=pl.DeviceIdType.MESH)

    rest = n_col - 2
    end_a = 2 * n_row
    end_d = end_a + 2 * EARLY * n_row
    end_t = end_d + rest * n_row

    def tile_of(s):
        t = jnp.maximum(jnp.where(s < end_t, s - end_a, s - end_t + 2 * EARLY * n_row), 0)
        i = t // n_row
        c_d = 2 * z_order(i // 2) + jnp.where(i % 2 == 0, 1 - k, k)
        v = jnp.maximum(s - end_d, 0)
        a_b = (r + 1 + v // rest) % n_row
        jj = v % rest
        c_b = 2 * ((z + 1 + jj // 2) % nz) + jj % 2
        in_t = (s >= end_d) & (s < end_t)
        a = jnp.where(in_t, a_b, jnp.where(s < end_a, s % n_row, t % n_row))
        col = jnp.where(in_t, c_b, jnp.where(s >= end_a, c_d, jnp.where(s < n_row, c, other)))
        return a, col

    def z_order(i):
        i = jnp.clip(i, 0, last)
        return jnp.where(z < nz // 2, last - i, i)

    total = 2 * n_row * n_col

    def tile_copy(s):
        a, col = tile_of(s)
        return pltpu.make_async_copy(
            G.at[pl.ds(pl.multiple_of(a * g, g), g), pl.ds(pl.multiple_of(col * g, g), g)],
            gbuf.at[s % NB],
            gsem.at[s % NB],
        )

    def next_tile(s):
        tile_copy(s).wait()

        @pl.when(s + NB - 1 < total)
        def _():
            tile_copy(s + NB - 1).start()

        a, col = tile_of(s)
        return a, col, gbuf[s % NB]

    for s in range(NB - 1):
        tile_copy(s).start()

    barrier = pltpu.get_barrier_semaphore()
    for d in range(1, n_row):
        pl.semaphore_signal(barrier, inc=1, **dev((r + d) % n_row, c))
    for d in range(1, n_col):
        pl.semaphore_signal(barrier, inc=1, **dev(r, (c + d) % n_col))
    pl.semaphore_wait(barrier, n_row + n_col - 2)

    def col_send(d):
        return pltpu.make_async_remote_copy(
            panel_t, colp.at[r], cs.at[d], cr.at[d], **dev((r + d) % n_row, c)
        )

    def block_send(h, way, src):
        zb = z - (h - 1) if way == 0 else z + (h - 1)
        slot = 2 * zb + k
        return pltpu.make_async_remote_copy(
            rowp.at[slot] if src is None else src,
            rowp.at[slot],
            zs.at[way, h],
            zr.at[way, h],
            **dev(r, c + 2 if way == 0 else c - 2),
        )

    def pair_send(zb, src):
        slot = 2 * zb + k
        return pltpu.make_async_remote_copy(
            rowp.at[slot] if src is None else src, rowp.at[slot], ps.at[zb], prr.at[zb], **dev(r, other)
        )

    pair_send(z, panel).start()

    @pl.when(z < last)
    def _():
        block_send(1, 0, panel).start()

    @pl.when(z > 0)
    def _():
        block_send(1, 1, panel).start()

    for d in range(1, n_row):
        col_send(d).start()

    def relay(h):
        for way in range(2):
            zb = z - h if way == 0 else z + h
            have = (zb >= 0) if way == 0 else (zb <= last)
            onward = (z < last) if way == 0 else (z > 0)

            @pl.when(have)
            def _():
                pltpu.make_async_remote_copy(
                    panel, rowp.at[2 * zb + k], zs.at[way, h], zr.at[way, h], **dev(r, other)
                ).wait_recv()
                pair_send(zb, None).start()

                @pl.when(onward)
                def _():
                    block_send(h + 1, way, None).start()

    rowp[c] = panel[...]
    colp[r] = panel_t[...]

    def zero(a, carry):
        tacc[a] = jnp.zeros((g, panel.shape[1]), F32)
        return carry

    lax.fori_loop(0, n_row, zero, 0)

    def t_step(s, carry):
        a, col, tile = next_tile(s)
        tacc[a] += dot(tile, rowp[col])
        return carry

    lax.fori_loop(0, n_row, t_step, 0)

    def pair_wait(zb):
        pltpu.make_async_remote_copy(
            panel, rowp.at[2 * zb + 1 - k], ps.at[zb], prr.at[zb], **dev(r, other)
        ).wait_recv()

    pair_wait(z)
    lax.fori_loop(n_row, 2 * n_row, t_step, 0)
    invert_blocks(low, inv_out)
    own_t[...] = jnp.zeros(own_t.shape, F32)
    left_over = pg[...]
    for _ in range(3):
        piece = left_over.astype(BF16)
        own_t[...] += dot(panel_t[...], piece)
        left_over = left_over - piece.astype(F32)
    relay(1)
    for d in range(1, n_row):
        pltpu.make_async_remote_copy(
            panel_t, colp.at[(r + n_row - d) % n_row], cs.at[d], cr.at[d], **dev((r + d) % n_row, c)
        ).wait_recv()

    def part_send(zb, slot):
        return pltpu.make_async_remote_copy(
            dpart.at[slot], pr.at[zb], ds.at[slot], dr.at[zb], **dev(r, other)
        )

    def sum_send(way, zb):
        return pltpu.make_async_remote_copy(
            dsum.at[zb], rl.at[way, zb], rs.at[way, zb], rr.at[way, zb],
            **dev(r, c + 2 if way == 0 else c - 2),
        )

    def add_in(dst, src):
        cp = pltpu.make_async_copy(src, stage, lsem)
        cp.start()
        cp.wait()
        dst[...] += stage[...]

    def presum(i):
        zb = z_order(i)
        part_send(zb, i % 2).wait_recv()
        add_in(dsum.at[zb], pr.at[zb])

        @pl.when((z == 0) & (zb > 0))
        def _():
            sum_send(0, zb).start()

        @pl.when((z == last) & (zb < last))
        def _():
            sum_send(1, zb).start()

    def d_into(base, ref):
        def step(j, carry):
            a, col, tile = next_tile(base + j)
            part = dot(colp[a], tile)

            @pl.when(j == 0)
            def _():
                ref[...] = part

            @pl.when(j > 0)
            def _():
                ref[...] += part

            return carry

        lax.fori_loop(0, n_row, step, 0)

    def d_pair(i, base):
        zb = z_order(i)
        slot = i % 2
        if i >= 2:
            part_send(z_order(i - 2), slot).wait_send()
        d_into(base, dpart.at[slot])
        part_send(zb, slot).start()
        d_into(base + n_row, dsum.at[zb])
        presum(i)

    for i in range(EARLY):
        d_pair(i, end_a + 2 * i * n_row)
        if i + 2 < nz:
            relay(i + 2)
    for h in range(EARLY + 2, nz):
        relay(h)

    def wait_others(d, carry):
        pair_wait((z + d) % nz)
        return carry

    lax.fori_loop(1, nz, wait_others, 0)

    def t_send(d):
        a = (r + d) % n_row
        return pltpu.make_async_remote_copy(
            tacc.at[a], tr.at[r], ts.at[d], trs.at[d], **dev(a, c)
        )

    for i in range(n_row):
        lax.fori_loop(end_d + i * rest, end_d + (i + 1) * rest, t_step, 0)
        if i == 0:
            t_send(1).start()

    q_out[...] = jnp.zeros(q_out.shape, F32)

    def q_step(a, carry):
        t = tacc[a]
        hi = t.astype(BF16)
        lo = (t - hi.astype(F32)).astype(BF16)
        q_out[...] += dot(colp[a], hi) + dot(colp[a], lo)
        return carry

    lax.fori_loop(0, n_row, q_step, 0)

    for n, (i, j) in enumerate(lower_blocks(q_out.shape[0] // BLK)):
        bi, bj = slice(i * BLK, (i + 1) * BLK), slice(j * BLK, (j + 1) * BLK)
        sx[n * BLK : (n + 1) * BLK, :] = (own_t[bj, bi] - q_out[bj, bi]).T - q_out[bi, bj]

    remote = pltpu.make_async_remote_copy
    length = s_row.shape[0]
    short = s_col.shape[0]

    def longs(ref, row):
        return ref.at[pl.ds(pl.multiple_of(row * length, 8), length)]

    def shorts(ref, col, row=None):
        start = col * short if row is None else row * length + col * short
        return ref.at[pl.ds(pl.multiple_of(start, 8), short)]

    row_at = lambda d: (r + d) % n_row
    col_at = lambda d: (c + d) % n_col
    one = [
        remote(longs(sx, row_at(d)), s_in.at[d], s1.at[d], r1.at[d], **dev(row_at(d), c))
        for d in range(1, n_row)
    ]
    two = [
        remote(shorts(s_row, col_at(d)), s_in.at[0, pl.ds(d * short, short)], s2.at[d], r2.at[d],
               **dev(r, col_at(d)))
        for d in range(1, n_col)
    ]
    three = [
        remote(shorts(s_all, c, r), shorts(s_all, c, r), s3.at[d], r3.at[d], **dev(r, col_at(d)))
        for d in range(1, n_col)
    ]
    four = [
        remote(longs(s_all, r), longs(s_all, r), s4.at[d], r4.at[d], **dev(row_at(d), c))
        for d in range(1, n_row)
    ]

    def start_all(copies):
        for cp in copies:
            cp.start()

    start_all(one)
    for d in range(2, n_row):
        t_send(d).start()

    for i in range(EARLY, nz):
        d_pair(i, end_t + 2 * (i - EARLY) * n_row)

    def hop(way, zb):
        sum_wait = pltpu.make_async_remote_copy(
            stage, rl.at[way, zb], rs.at[way, zb], rr.at[way, zb], **dev(r, other)
        )
        sum_wait.wait_recv()
        add_in(dsum.at[zb], rl.at[way, zb])

    def pass_up(zb):
        @pl.when((z > 0) & (zb > z))
        def _():
            hop(0, zb)
            sum_send(0, zb).start()

    def pass_down(zb, side):
        @pl.when((z < last) & (zb < z) & side)
        def _():
            hop(1, zb)
            sum_send(1, zb).start()

    for q in range(nz):
        if q == 1:
            s_row[...] = longs(sx, r)[...]
            for d in range(1, n_row):
                one[d - 1].wait_recv()
                s_row[...] += s_in[d]
            start_all(two)
        pass_down(q, z >= nz // 2)
        pass_up(last - q)
        pass_down(q, z < nz // 2)

    s_col[...] = shorts(s_row, c)[...]
    for d in range(1, n_col):
        two[d - 1].wait_recv()
        s_col[...] += s_in[0, d * short : (d + 1) * short, :]
    shorts(s_all, c, r)[...] = s_col[...]
    start_all(three)

    def fetch(src, dst):
        cp = pltpu.make_async_copy(src, dst, lsem)
        cp.start()
        cp.wait()

    tacc[r] = pg[...] - tacc[r]
    tbuf = tacc.at[(r + 1) % n_row]
    for d in range(1, n_row):
        t_send(d).wait_send()
    for d in range(1, n_row):
        src = (r + n_row - d) % n_row
        pltpu.make_async_remote_copy(
            tacc.at[src], tr.at[src], ts.at[d], trs.at[d], **dev((r + d) % n_row, c)
        ).wait_recv()
        fetch(tr.at[src], tbuf)
        tacc[r] -= tbuf[...]

    for d in range(1, n_col):
        remote(
            shorts(s_all, c, r), shorts(s_all, col_at(n_col - d), r), s3.at[d], r3.at[d],
            **dev(r, col_at(d)),
        ).wait_recv()
    start_all(four)

    @pl.when(z > 0)
    def _():
        hop(0, z)

    @pl.when(z < last)
    def _():
        hop(1, z)

    adj_out[...] = right_blocks(tacc[r] - dsum[z].T, low, inv_out)
    for d in range(1, n_row):
        remote(
            longs(s_all, r), longs(s_all, row_at(n_row - d)), s4.at[d], r4.at[d],
            **dev(row_at(d), c),
        ).wait_recv()
    blocks = q_out.shape[0] // BLK
    q_out[...] = jnp.zeros(q_out.shape, F32)
    for n, (i, j) in enumerate(lower_blocks(blocks)):
        q_out[i * BLK : (i + 1) * BLK, j * BLK : (j + 1) * BLK] = s_all[n * BLK : (n + 1) * BLK, :]
    diag_kernel(q_out, dg, low, inv_out, diag_out)
    for cp in one + two + three + four:
        cp.wait_send()

    for d in range(1, n_row):
        col_send(d).wait_send()
    for way in range(2):
        for h in range(1, nz):
            zb = z - (h - 1) if way == 0 else z + (h - 1)
            sent = ((zb >= 0) & (z < last)) if way == 0 else ((zb <= last) & (z > 0))

            @pl.when(sent)
            def _():
                block_send(h, way, panel).wait_send()

    for zb in range(nz):
        pair_send(zb, panel).wait_send()
        sent_up = z < zb
        sent_down = z > zb

        @pl.when(sent_up)
        def _():
            sum_send(0, zb).wait_send()

        @pl.when(sent_down)
        def _():
            sum_send(1, zb).wait_send()

    for i in range(max(nz - 2, 0), nz):
        part_send(z_order(i), i % 2).wait_send()


def main_call(G, panel, pg, low, dg, n_row, n_col):
    g, b = panel.shape
    nz = n_col // 2
    entries = len(lower_blocks(b // BLK)) * BLK
    vm = pl.BlockSpec(memory_space=pltpu.VMEM)
    hbm = pl.BlockSpec(memory_space=pl.ANY)
    dma = pltpu.SemaphoreType.DMA
    sds = jax.ShapeDtypeStruct
    sizes = [(NB,), (n_row,), (n_row,), (2, nz + 1), (2, nz + 1), (nz,), (nz,), (2,), (nz,),
             (2, nz), (2, nz), (n_row,), (n_row,), (n_row,), (n_row,), (n_col,), (n_col,), (n_col,), (n_col,),
             (n_row,), (n_row,)]
    flops = 4 * G.shape[0] * G.shape[1] * b
    outs = pl.pallas_call(
        functools.partial(main_kernel, n_row, n_col),
        out_shape=[
            sds((g, b), F32), sds((b, b), F32),
            sds((nz, b, g), F32), sds((2, nz, b, g), F32), sds((n_row, g, b), F32),
        ],
        in_specs=[hbm, vm, vm, vm, vm, vm],
        out_specs=[vm, vm, hbm, hbm, hbm],
        scratch_shapes=[
            pltpu.VMEM((n_row, b, g), BF16),
            pltpu.VMEM((n_col, g, b), BF16),
            pltpu.VMEM((NB, g, g), BF16),
            pltpu.VMEM((n_row, g, b), F32),
            pltpu.VMEM((nz, b, g), F32),
            pltpu.VMEM((2, b, g), F32),
            pltpu.VMEM((b, g), F32),
            pltpu.VMEM((b, b), F32),
            pltpu.VMEM((b // BLK, BLK, BLK), F32),
            pltpu.VMEM((b, b), F32),
            pltpu.VMEM((entries, BLK), F32),
            pltpu.VMEM((n_row, entries // n_row, BLK), F32),
            pltpu.VMEM((entries // n_row, BLK), F32),
            pltpu.VMEM((entries // n_row // n_col, BLK), F32),
            pltpu.VMEM((entries, BLK), F32),
        ]
        + [dma(s) for s in sizes]
        + [dma],
        compiler_params=pltpu.CompilerParams(
            collective_id=0, has_side_effects=True, vmem_limit_bytes=VMEM_LIMIT
        ),
        cost_estimate=pl.CostEstimate(flops=flops, bytes_accessed=4 * G.size, transcendentals=0),
    )(G, panel, panel.T, pg, low, dg)
    return tuple(outs[:2])


def right_blocks(rhs, low, inv):
    n = low.shape[0] // BLK
    part = lambda j: slice(j * BLK, (j + 1) * BLK)
    xs = [None] * n
    for j in reversed(range(n)):
        acc = rhs[:, part(j)]
        if j < n - 1:
            done = jnp.concatenate(xs[j + 1 :], axis=1)
            acc = acc - dot(done, low[(j + 1) * BLK :, part(j)], precision=HI)
        xs[j] = dot(acc, inv[j], precision=HI)
    return jnp.concatenate(xs, axis=1)


def left_blocks(rhs, low, inv):
    n = low.shape[0] // BLK
    part = lambda j: slice(j * BLK, (j + 1) * BLK)
    xs = [None] * n
    for j in reversed(range(n)):
        acc = rhs[part(j), :]
        if j < n - 1:
            done = jnp.concatenate(xs[j + 1 :], axis=0)
            acc = acc - dot(low[(j + 1) * BLK :, part(j)], done, 0, 0, precision=HI)
        xs[j] = dot(inv[j], acc, 0, 0, precision=HI)
    return jnp.concatenate(xs, axis=0)


def panel_kernel(t_ref, dt_ref, low, inv, out):
    out[...] = right_blocks(t_ref[...] - dt_ref[...].T, low[...], inv[...])


def diag_kernel(s_ref, dg, low, inv, out):
    rows = lax.broadcasted_iota(jnp.int32, low.shape, 0)
    cols = lax.broadcasted_iota(jnp.int32, low.shape, 1)
    lower, inverse = jnp.where(rows >= cols, low[...], 0.0), inv[...]
    diag_new = dg[...] - left_blocks(s_ref[...], lower, inverse)
    inner = dot(lower, jnp.where(rows >= cols, diag_new, 0.0), 0, 0, precision=HI)
    inner = inner * jnp.where(rows > cols, 1.0, jnp.where(rows == cols, 0.5, 0.0))
    right = right_blocks(left_blocks(inner, lower, inverse), lower, inverse)
    out[...] = 0.5 * (right + right.T)


def local_call(body, shape, *args):
    vm = pl.BlockSpec(memory_space=pltpu.VMEM)
    return pl.pallas_call(
        body,
        out_shape=jax.ShapeDtypeStruct(shape, F32),
        in_specs=[vm] * len(args),
        out_specs=vm,
        compiler_params=pltpu.CompilerParams(vmem_limit_bytes=48_000_000),
    )(*args)


def plain_products(block, panel, panel_grad, lower):
    col_panel = lax.all_gather(panel, "row", axis=0, tiled=True)
    row_panel = lax.all_gather(panel, "col", axis=0, tiled=True)
    direct = lax.psum_scatter(dot(block, col_panel, 0, 0), "col", scatter_dimension=0, tiled=True)
    part = dot(block, row_panel)
    transposed = lax.psum_scatter(part, "row", scatter_dimension=0, tiled=True)
    high = part.astype(BF16)
    q = dot(col_panel, high, 0, 0) + dot(col_panel, (part - high.astype(F32)).astype(BF16), 0, 0)
    inv = local_call(invert_blocks, (lower.shape[0] // BLK, BLK, BLK), lower)
    return direct.T, panel_grad - transposed, q, inv


def on_device(n_row, n_col, trailing_grad, panel, panel_grad, diag_factor, diag_grad):
    local_flip = trailing_grad.reshape(-1, trailing_grad.shape[3])
    g, b = panel.shape
    shares = len(lower_blocks(b // BLK)) * BLK % (8 * n_row * n_col)
    if g % 128 == 0 and shares == 0 and n_col % 2 == 0 and n_col >= 4:
        return main_call(local_flip, panel, panel_grad, diag_factor, diag_grad, n_row, n_col)
    lower = jnp.tril(diag_factor)
    dt, t, q, inv = plain_products(local_flip, panel, panel_grad, lower)
    own = dot(panel_grad, panel.astype(F32), 0, 0, precision=HI)
    total = lax.psum(own - q - q.T, ("row", "col"))
    panel_adj = local_call(panel_kernel, panel_grad.shape, t, dt, lower, inv)
    diag_adj = local_call(diag_kernel, lower.shape, total, diag_grad, lower, inv)
    return (panel_adj, diag_adj)


def solution(mesh):
    in_specs = (
        P(None, "col", None, "row"),
        P(("row", "col"), None),
        P(("row", "col"), None),
        P(),
        P(),
    )
    out_specs = (P(("row", "col"), None), P())
    body = functools.partial(on_device, mesh.shape["row"], mesh.shape["col"])
    return jax.shard_map(body, mesh=mesh, in_specs=in_specs, out_specs=out_specs, check_vma=False)
```

```python
import functools

import jax
import jax.numpy as jnp
from jax import lax
from jax.experimental import pallas as pl
from jax.experimental.pallas import tpu as pltpu
from jax.sharding import PartitionSpec as P

F32, BF16 = jnp.float32, jnp.bfloat16
VMEM_LIMIT = 66_000_000
NB = 4
EARLY = 2
BLK = 128
HI = lax.Precision.HIGHEST


def dot(a, b, ca=1, cb=0, precision=None):
    return lax.dot_general(
        a, b, (((ca,), (cb,)), ((), ())), precision=precision, preferred_element_type=F32
    )


def lower_blocks(count):
    return [(i, j) for i in range(count) for j in range(i + 1)]


def invert_blocks(l_ref, inv_ref):
    rows = lax.broadcasted_iota(jnp.int32, (BLK, BLK), 0)
    cols = lax.broadcasted_iota(jnp.int32, (BLK, BLK), 1)
    count = l_ref.shape[0] // BLK
    for j in range(count):
        block = l_ref[j * BLK : (j + 1) * BLK, j * BLK : (j + 1) * BLK]
        inv_ref[j] = jnp.where(rows == cols, 1.0 / jnp.where(rows == cols, block, 1.0), 0.0)

    def level(k, carry):
        same = (rows >> (k + 1)) == (cols >> (k + 1))
        mask = same & (((rows >> k) & 1) == 1) & (((cols >> k) & 1) == 0)
        for j in range(count):
            block = l_ref[j * BLK : (j + 1) * BLK, j * BLK : (j + 1) * BLK]
            x = inv_ref[j]
            y = dot(jnp.where(mask, block, 0.0), x, precision=HI)
            inv_ref[j] = x - dot(x, y, precision=HI)
        return carry

    lax.fori_loop(0, BLK.bit_length() - 1, level, 0)


def main_kernel(
    n_row, n_col, G, panel, panel_t, pg, low,
    dg, adj_out, diag_out, pr, rl, tr,
    colp, rowp, gbuf, tacc, dsum, dpart, stage, q_out, inv_out, own_t, sx, s_in, s_row, s_col, s_all,
    gsem, cs, cr, zs, zr, ps, prr, ds, dr, rs, rr, ts, trs, s1, r1, s2, r2, s3, r3, s4, r4, lsem,
):
    nz = n_col // 2
    r, c = lax.axis_index("row"), lax.axis_index("col")
    z, k = c // 2, c % 2
    other = 2 * z + 1 - k
    g = panel.shape[0]
    last = nz - 1

    def dev(row, col):
        return dict(device_id=(row, col), device_id_type=pl.DeviceIdType.MESH)

    rest = n_col - 2
    end_a = 2 * n_row
    end_d = end_a + 2 * EARLY * n_row
    end_t = end_d + rest * n_row

    def tile_of(s):
        t = jnp.maximum(jnp.where(s < end_t, s - end_a, s - end_t + 2 * EARLY * n_row), 0)
        i = t // n_row
        c_d = 2 * z_order(i // 2) + jnp.where(i % 2 == 0, 1 - k, k)
        v = jnp.maximum(s - end_d, 0)
        a_b = (r + 1 + v // rest) % n_row
        jj = v % rest
        c_b = 2 * ((z + 1 + jj // 2) % nz) + jj % 2
        in_t = (s >= end_d) & (s < end_t)
        a = jnp.where(in_t, a_b, jnp.where(s < end_a, s % n_row, t % n_row))
        col = jnp.where(in_t, c_b, jnp.where(s >= end_a, c_d, jnp.where(s < n_row, c, other)))
        return a, col

    def z_order(i):
        i = jnp.clip(i, 0, last)
        return jnp.where(z < nz // 2, last - i, i)

    total = 2 * n_row * n_col

    def tile_copy(s):
        a, col = tile_of(s)
        return pltpu.make_async_copy(
            G.at[pl.ds(pl.multiple_of(a * g, g), g), pl.ds(pl.multiple_of(col * g, g), g)],
            gbuf.at[s % NB],
            gsem.at[s % NB],
        )

    def next_tile(s):
        tile_copy(s).wait()

        @pl.when(s + NB - 1 < total)
        def _():
            tile_copy(s + NB - 1).start()

        a, col = tile_of(s)
        return a, col, gbuf[s % NB]

    for s in range(NB - 1):
        tile_copy(s).start()

    barrier = pltpu.get_barrier_semaphore()
    for d in range(1, n_row):
        pl.semaphore_signal(barrier, inc=1, **dev((r + d) % n_row, c))
    for d in range(1, n_col):
        pl.semaphore_signal(barrier, inc=1, **dev(r, (c + d) % n_col))
    pl.semaphore_wait(barrier, n_row + n_col - 2)

    def col_send(d):
        return pltpu.make_async_remote_copy(
            panel_t, colp.at[r], cs.at[d], cr.at[d], **dev((r + d) % n_row, c)
        )

    def block_send(h, way, src):
        zb = z - (h - 1) if way == 0 else z + (h - 1)
        slot = 2 * zb + k
        return pltpu.make_async_remote_copy(
            rowp.at[slot] if src is None else src,
            rowp.at[slot],
            zs.at[way, h],
            zr.at[way, h],
            **dev(r, c + 2 if way == 0 else c - 2),
        )

    def pair_send(zb, src):
        slot = 2 * zb + k
        return pltpu.make_async_remote_copy(
            rowp.at[slot] if src is None else src, rowp.at[slot], ps.at[zb], prr.at[zb], **dev(r, other)
        )

    pair_send(z, panel).start()

    @pl.when(z < last)
    def _():
        block_send(1, 0, panel).start()

    @pl.when(z > 0)
    def _():
        block_send(1, 1, panel).start()

    for d in range(1, n_row):
        col_send(d).start()

    def relay(h):
        for way in range(2):
            zb = z - h if way == 0 else z + h
            have = (zb >= 0) if way == 0 else (zb <= last)
            onward = (z < last) if way == 0 else (z > 0)

            @pl.when(have)
            def _():
                pltpu.make_async_remote_copy(
                    panel, rowp.at[2 * zb + k], zs.at[way, h], zr.at[way, h], **dev(r, other)
                ).wait_recv()
                pair_send(zb, None).start()

                @pl.when(onward)
                def _():
                    block_send(h + 1, way, None).start()

    rowp[c] = panel[...]
    colp[r] = panel_t[...]

    def zero(a, carry):
        tacc[a] = jnp.zeros((g, panel.shape[1]), F32)
        return carry

    lax.fori_loop(0, n_row, zero, 0)

    def t_step(s, carry):
        a, col, tile = next_tile(s)
        tacc[a] += dot(tile, rowp[col])
        return carry

    lax.fori_loop(0, n_row, t_step, 0)

    def pair_wait(zb):
        pltpu.make_async_remote_copy(
            panel, rowp.at[2 * zb + 1 - k], ps.at[zb], prr.at[zb], **dev(r, other)
        ).wait_recv()

    pair_wait(z)
    lax.fori_loop(n_row, 2 * n_row, t_step, 0)
    invert_blocks(low, inv_out)
    own_t[...] = jnp.zeros(own_t.shape, F32)
    left_over = pg[...]
    for _ in range(3):
        piece = left_over.astype(BF16)
        own_t[...] += dot(panel_t[...], piece)
        left_over = left_over - piece.astype(F32)
    relay(1)
    for d in range(1, n_row):
        pltpu.make_async_remote_copy(
            panel_t, colp.at[(r + n_row - d) % n_row], cs.at[d], cr.at[d], **dev((r + d) % n_row, c)
        ).wait_recv()

    def part_send(zb, slot):
        return pltpu.make_async_remote_copy(
            dpart.at[slot], pr.at[zb], ds.at[slot], dr.at[zb], **dev(r, other)
        )

    def sum_send(way, zb):
        return pltpu.make_async_remote_copy(
            dsum.at[zb], rl.at[way, zb], rs.at[way, zb], rr.at[way, zb],
            **dev(r, c + 2 if way == 0 else c - 2),
        )

    def add_in(dst, src):
        cp = pltpu.make_async_copy(src, stage, lsem)
        cp.start()
        cp.wait()
        dst[...] += stage[...]

    def presum(i):
        zb = z_order(i)
        part_send(zb, i % 2).wait_recv()
        add_in(dsum.at[zb], pr.at[zb])

        @pl.when((z == 0) & (zb > 0))
        def _():
            sum_send(0, zb).start()

        @pl.when((z == last) & (zb < last))
        def _():
            sum_send(1, zb).start()

    def d_into(base, ref):
        def step(j, carry):
            a, col, tile = next_tile(base + j)
            part = dot(colp[a], tile)

            @pl.when(j == 0)
            def _():
                ref[...] = part

            @pl.when(j > 0)
            def _():
                ref[...] += part

            return carry

        lax.fori_loop(0, n_row, step, 0)

    def d_pair(i, base, between=None):
        zb = z_order(i)
        slot = i % 2
        if i >= 2:
            part_send(z_order(i - 2), slot).wait_send()
        d_into(base, dpart.at[slot])
        part_send(zb, slot).start()
        d_into(base + n_row, dsum.at[zb])
        if between is not None:
            between()
        presum(i)

    for i in range(EARLY):
        d_pair(i, end_a + 2 * i * n_row)
        if i + 2 < nz:
            relay(i + 2)
    for h in range(EARLY + 2, nz):
        relay(h)

    def wait_others(d, carry):
        pair_wait((z + d) % nz)
        return carry

    lax.fori_loop(1, nz, wait_others, 0)

    def t_send(d):
        a = (r + d) % n_row
        return pltpu.make_async_remote_copy(
            tacc.at[a], tr.at[r], ts.at[d], trs.at[d], **dev(a, c)
        )

    for i in range(n_row):
        lax.fori_loop(end_d + i * rest, end_d + (i + 1) * rest, t_step, 0)
        if i == 0:
            t_send(1).start()

    q_out[...] = jnp.zeros(q_out.shape, F32)

    def q_step(a, carry):
        t = tacc[a]
        hi = t.astype(BF16)
        lo = (t - hi.astype(F32)).astype(BF16)
        q_out[...] += dot(colp[a], hi) + dot(colp[a], lo)
        return carry

    lax.fori_loop(0, n_row, q_step, 0)

    for n, (i, j) in enumerate(lower_blocks(q_out.shape[0] // BLK)):
        bi, bj = slice(i * BLK, (i + 1) * BLK), slice(j * BLK, (j + 1) * BLK)
        sx[n * BLK : (n + 1) * BLK, :] = (own_t[bj, bi] - q_out[bj, bi]).T - q_out[bi, bj]

    remote = pltpu.make_async_remote_copy
    length = s_row.shape[0]
    short = s_col.shape[0]

    def longs(ref, row):
        return ref.at[pl.ds(pl.multiple_of(row * length, 8), length)]

    def shorts(ref, col, row=None):
        start = col * short if row is None else row * length + col * short
        return ref.at[pl.ds(pl.multiple_of(start, 8), short)]

    row_at = lambda d: (r + d) % n_row
    col_at = lambda d: (c + d) % n_col
    one = [
        remote(longs(sx, row_at(d)), s_in.at[d], s1.at[d], r1.at[d], **dev(row_at(d), c))
        for d in range(1, n_row)
    ]
    two = [
        remote(shorts(s_row, col_at(d)), s_in.at[0, pl.ds(d * short, short)], s2.at[d], r2.at[d],
               **dev(r, col_at(d)))
        for d in range(1, n_col)
    ]
    three = [
        remote(shorts(s_all, c, r), shorts(s_all, c, r), s3.at[d], r3.at[d], **dev(r, col_at(d)))
        for d in range(1, n_col)
    ]
    four = [
        remote(longs(s_all, r), longs(s_all, r), s4.at[d], r4.at[d], **dev(row_at(d), c))
        for d in range(1, n_row)
    ]

    def start_all(copies):
        for cp in copies:
            cp.start()

    start_all(one)
    for d in range(2, n_row):
        t_send(d).start()

    def along_col():
        s_row[...] = longs(sx, r)[...]
        for d in range(1, n_row):
            one[d - 1].wait_recv()
            s_row[...] += s_in[d]
        start_all(two)

    for i in range(EARLY, nz):
        d_pair(i, end_t + 2 * (i - EARLY) * n_row, along_col if i == EARLY else None)
    if nz <= EARLY:
        along_col()

    def hop(way, zb):
        sum_wait = pltpu.make_async_remote_copy(
            stage, rl.at[way, zb], rs.at[way, zb], rr.at[way, zb], **dev(r, other)
        )
        sum_wait.wait_recv()
        add_in(dsum.at[zb], rl.at[way, zb])

    def pass_up(zb):
        @pl.when((z > 0) & (zb > z))
        def _():
            hop(0, zb)
            sum_send(0, zb).start()

    def pass_down(zb, side):
        @pl.when((z < last) & (zb < z) & side)
        def _():
            hop(1, zb)
            sum_send(1, zb).start()

    for q in range(nz):
        pass_down(q, z >= nz // 2)
        pass_up(last - q)
        pass_down(q, z < nz // 2)

    s_col[...] = shorts(s_row, c)[...]
    for d in range(1, n_col):
        two[d - 1].wait_recv()
        s_col[...] += s_in[0, d * short : (d + 1) * short, :]
    shorts(s_all, c, r)[...] = s_col[...]
    start_all(three)

    for d in range(1, n_col):
        remote(
            shorts(s_all, c, r), shorts(s_all, col_at(n_col - d), r), s3.at[d], r3.at[d],
            **dev(r, col_at(d)),
        ).wait_recv()
    start_all(four)

    def fetch(src, dst):
        cp = pltpu.make_async_copy(src, dst, lsem)
        cp.start()
        cp.wait()

    tacc[r] = pg[...] - tacc[r]
    tbuf = tacc.at[(r + 1) % n_row]
    for d in range(1, n_row):
        t_send(d).wait_send()
    for d in range(1, n_row):
        src = (r + n_row - d) % n_row
        pltpu.make_async_remote_copy(
            tacc.at[src], tr.at[src], ts.at[d], trs.at[d], **dev((r + d) % n_row, c)
        ).wait_recv()
        fetch(tr.at[src], tbuf)
        tacc[r] -= tbuf[...]

    @pl.when(z > 0)
    def _():
        hop(0, z)

    @pl.when(z < last)
    def _():
        hop(1, z)

    adj_out[...] = right_blocks(tacc[r] - dsum[z].T, low, inv_out)
    for d in range(1, n_row):
        remote(
            longs(s_all, r), longs(s_all, row_at(n_row - d)), s4.at[d], r4.at[d],
            **dev(row_at(d), c),
        ).wait_recv()
    blocks = q_out.shape[0] // BLK
    q_out[...] = jnp.zeros(q_out.shape, F32)
    for n, (i, j) in enumerate(lower_blocks(blocks)):
        q_out[i * BLK : (i + 1) * BLK, j * BLK : (j + 1) * BLK] = s_all[n * BLK : (n + 1) * BLK, :]
    diag_kernel(q_out, dg, low, inv_out, diag_out)
    for cp in one + two + three + four:
        cp.wait_send()

    for d in range(1, n_row):
        col_send(d).wait_send()
    for way in range(2):
        for h in range(1, nz):
            zb = z - (h - 1) if way == 0 else z + (h - 1)
            sent = ((zb >= 0) & (z < last)) if way == 0 else ((zb <= last) & (z > 0))

            @pl.when(sent)
            def _():
                block_send(h, way, panel).wait_send()

    for zb in range(nz):
        pair_send(zb, panel).wait_send()
        sent_up = z < zb
        sent_down = z > zb

        @pl.when(sent_up)
        def _():
            sum_send(0, zb).wait_send()

        @pl.when(sent_down)
        def _():
            sum_send(1, zb).wait_send()

    for i in range(max(nz - 2, 0), nz):
        part_send(z_order(i), i % 2).wait_send()


def main_call(G, panel, pg, low, dg, n_row, n_col):
    g, b = panel.shape
    nz = n_col // 2
    entries = len(lower_blocks(b // BLK)) * BLK
    vm = pl.BlockSpec(memory_space=pltpu.VMEM)
    hbm = pl.BlockSpec(memory_space=pl.ANY)
    dma = pltpu.SemaphoreType.DMA
    sds = jax.ShapeDtypeStruct
    sizes = [(NB,), (n_row,), (n_row,), (2, nz + 1), (2, nz + 1), (nz,), (nz,), (2,), (nz,),
             (2, nz), (2, nz), (n_row,), (n_row,), (n_row,), (n_row,), (n_col,), (n_col,), (n_col,), (n_col,),
             (n_row,), (n_row,)]
    flops = 4 * G.shape[0] * G.shape[1] * b
    outs = pl.pallas_call(
        functools.partial(main_kernel, n_row, n_col),
        out_shape=[
            sds((g, b), F32), sds((b, b), F32),
            sds((nz, b, g), F32), sds((2, nz, b, g), F32), sds((n_row, g, b), F32),
        ],
        in_specs=[hbm, vm, vm, vm, vm, vm],
        out_specs=[vm, vm, hbm, hbm, hbm],
        scratch_shapes=[
            pltpu.VMEM((n_row, b, g), BF16),
            pltpu.VMEM((n_col, g, b), BF16),
            pltpu.VMEM((NB, g, g), BF16),
            pltpu.VMEM((n_row, g, b), F32),
            pltpu.VMEM((nz, b, g), F32),
            pltpu.VMEM((2, b, g), F32),
            pltpu.VMEM((b, g), F32),
            pltpu.VMEM((b, b), F32),
            pltpu.VMEM((b // BLK, BLK, BLK), F32),
            pltpu.VMEM((b, b), F32),
            pltpu.VMEM((entries, BLK), F32),
            pltpu.VMEM((n_row, entries // n_row, BLK), F32),
            pltpu.VMEM((entries // n_row, BLK), F32),
            pltpu.VMEM((entries // n_row // n_col, BLK), F32),
            pltpu.VMEM((entries, BLK), F32),
        ]
        + [dma(s) for s in sizes]
        + [dma],
        compiler_params=pltpu.CompilerParams(
            collective_id=0, has_side_effects=True, vmem_limit_bytes=VMEM_LIMIT
        ),
        cost_estimate=pl.CostEstimate(flops=flops, bytes_accessed=4 * G.size, transcendentals=0),
    )(G, panel, panel.T, pg, low, dg)
    return tuple(outs[:2])


def right_blocks(rhs, low, inv):
    n = low.shape[0] // BLK
    part = lambda j: slice(j * BLK, (j + 1) * BLK)
    xs = [None] * n
    for j in reversed(range(n)):
        acc = rhs[:, part(j)]
        if j < n - 1:
            done = jnp.concatenate(xs[j + 1 :], axis=1)
            acc = acc - dot(done, low[(j + 1) * BLK :, part(j)], precision=HI)
        xs[j] = dot(acc, inv[j], precision=HI)
    return jnp.concatenate(xs, axis=1)


def left_blocks(rhs, low, inv):
    n = low.shape[0] // BLK
    part = lambda j: slice(j * BLK, (j + 1) * BLK)
    xs = [None] * n
    for j in reversed(range(n)):
        acc = rhs[part(j), :]
        if j < n - 1:
            done = jnp.concatenate(xs[j + 1 :], axis=0)
            acc = acc - dot(low[(j + 1) * BLK :, part(j)], done, 0, 0, precision=HI)
        xs[j] = dot(inv[j], acc, 0, 0, precision=HI)
    return jnp.concatenate(xs, axis=0)


def panel_kernel(t_ref, dt_ref, low, inv, out):
    out[...] = right_blocks(t_ref[...] - dt_ref[...].T, low[...], inv[...])


def diag_kernel(s_ref, dg, low, inv, out):
    rows = lax.broadcasted_iota(jnp.int32, low.shape, 0)
    cols = lax.broadcasted_iota(jnp.int32, low.shape, 1)
    lower, inverse = jnp.where(rows >= cols, low[...], 0.0), inv[...]
    diag_new = dg[...] - left_blocks(s_ref[...], lower, inverse)
    inner = dot(lower, jnp.where(rows >= cols, diag_new, 0.0), 0, 0, precision=HI)
    inner = inner * jnp.where(rows > cols, 1.0, jnp.where(rows == cols, 0.5, 0.0))
    right = right_blocks(left_blocks(inner, lower, inverse), lower, inverse)
    out[...] = 0.5 * (right + right.T)


def local_call(body, shape, *args):
    vm = pl.BlockSpec(memory_space=pltpu.VMEM)
    return pl.pallas_call(
        body,
        out_shape=jax.ShapeDtypeStruct(shape, F32),
        in_specs=[vm] * len(args),
        out_specs=vm,
        compiler_params=pltpu.CompilerParams(vmem_limit_bytes=48_000_000),
    )(*args)


def plain_products(block, panel, panel_grad, lower):
    col_panel = lax.all_gather(panel, "row", axis=0, tiled=True)
    row_panel = lax.all_gather(panel, "col", axis=0, tiled=True)
    direct = lax.psum_scatter(dot(block, col_panel, 0, 0), "col", scatter_dimension=0, tiled=True)
    part = dot(block, row_panel)
    transposed = lax.psum_scatter(part, "row", scatter_dimension=0, tiled=True)
    high = part.astype(BF16)
    q = dot(col_panel, high, 0, 0) + dot(col_panel, (part - high.astype(F32)).astype(BF16), 0, 0)
    inv = local_call(invert_blocks, (lower.shape[0] // BLK, BLK, BLK), lower)
    return direct.T, panel_grad - transposed, q, inv


def on_device(n_row, n_col, trailing_grad, panel, panel_grad, diag_factor, diag_grad):
    local_flip = trailing_grad.reshape(-1, trailing_grad.shape[3])
    g, b = panel.shape
    shares = len(lower_blocks(b // BLK)) * BLK % (8 * n_row * n_col)
    if g % 128 == 0 and shares == 0 and n_col % 2 == 0 and n_col >= 4:
        return main_call(local_flip, panel, panel_grad, diag_factor, diag_grad, n_row, n_col)
    lower = jnp.tril(diag_factor)
    dt, t, q, inv = plain_products(local_flip, panel, panel_grad, lower)
    own = dot(panel_grad, panel.astype(F32), 0, 0, precision=HI)
    total = lax.psum(own - q - q.T, ("row", "col"))
    panel_adj = local_call(panel_kernel, panel_grad.shape, t, dt, lower, inv)
    diag_adj = local_call(diag_kernel, lower.shape, total, diag_grad, lower, inv)
    return (panel_adj, diag_adj)


def solution(mesh):
    in_specs = (
        P(None, "col", None, "row"),
        P(("row", "col"), None),
        P(("row", "col"), None),
        P(),
        P(),
    )
    out_specs = (P(("row", "col"), None), P())
    body = functools.partial(on_device, mesh.shape["row"], mesh.shape["col"])
    return jax.shard_map(body, mesh=mesh, in_specs=in_specs, out_specs=out_specs, check_vma=False)
```
